32 devices in a mesh: groups: 2 (over x), freq: 16 (over z, y, core).
Axes of the slice: x: 2, y: 2, z: 4, core: 2. Of those that a mesh axis runs over, the one named last changes fastest.
Arguments:
- volts: bfloat16 [256, 68608], P(('groups', 'freq')), parts along dimension 0, may hold values from -6 to 6
- filter_taps: float32 [4, 1024], replicated, may hold values from -3 to 3
- kernel: float32 [63], replicated, may hold values from -0.5 to 0.5
Outputs:
- smoothed: bfloat16 [512, 256, 128], P(None, ('groups', 'freq')), parts along dimension 1
The draws below stay inside these ranges and needn't reach their ends.
There are 2 independent parts, one for each index of `groups`. The reference program is written for one: setup_inputs(seed, part) draws one part's arguments, and reference() takes and returns one part's arrays. A program takes and returns all parts, laid end to end along the dimension named above; an argument that names none is the same for every part. Nothing has to cross between parts.
All inputs are finite; a program needn't handle non-finite values.
Results may differ from the reference program's by a relative error of at most 0.011.
Values may be sent and summed in bfloat16 or wider, within the bound.
A program may use at most 128 MiB of HBM per device.

```python
import jax
import jax.numpy as jnp
from jax import lax

CH = 512
FRAME = 1024
TAPS = 4
KERNEL = 63
SPEC = 64
INPUTS = 128
SAMPLES = 68608


def levels(key, extent, split, least, top_value):
    level, own = 1.0, jax.random.fold_in(key, 6)
    for position, shards_of in split:
        draws = jnp.exp(jax.random.uniform(jax.random.fold_in(own, position), (shards_of,), jnp.float32, least / len(split), top_value / len(split)))
        level = level * jnp.repeat(draws, extent[position] // shards_of).reshape([-1 if axis == position else 1 for axis in range(len(extent))])
    return level


def scatter_about(rng, dims, spread, bound, shards=(), kind=jnp.bfloat16):
    loudness = levels(rng, dims, shards, -0.22, 0.18) if shards else 1.0
    drawn = jax.random.normal(rng, dims, jnp.float32) * spread * loudness
    return jnp.minimum(jnp.maximum(drawn, -bound), bound).astype(kind)


def setup_inputs(seed: int = 0, part: int = 0) -> dict:
    seeds = jax.random.split(jax.random.key(seed), 4)
    part_keys = jax.random.split(jax.random.fold_in(seeds[3], part), 4)
    volts = scatter_about(part_keys[0], (INPUTS, SAMPLES), 1.0, 6.0, ((0, 16),))
    filter_taps = scatter_about(seeds[1], (TAPS, FRAME), 0.5, 3.0, (), jnp.float32)
    kernel = scatter_about(seeds[2], (KERNEL,), 0.125, 0.5, (), jnp.float32)
    return dict(volts=volts, filter_taps=filter_taps, kernel=kernel)


def make_table(frame, channels):
    rows = jnp.arange(frame, dtype=jnp.int32)
    cols = jnp.arange(channels, dtype=jnp.int32)
    phase = (2 * rows[:, None] + 1 + channels) * (2 * cols[None, :] + 1) % (8 * channels)
    angle = phase.astype(jnp.float32) * (jnp.pi / (4.0 * channels))
    return (jnp.cos(angle) * (1.0 / jnp.sqrt(jnp.float32(channels)))).astype(jnp.bfloat16)

def reference(volts, filter_taps, kernel):
    blocks = volts.reshape(INPUTS, SPEC + TAPS - 1, FRAME).astype(jnp.float32)
    filtered = jnp.zeros((INPUTS, SPEC, FRAME), jnp.float32)
    for tap in range(TAPS):
        filtered = filtered + filter_taps[tap][None, None, :] * blocks[:, tap:tap + SPEC, :]
    filtered = filtered.astype(jnp.bfloat16)
    table = make_table(FRAME, CH)
    chan = jnp.dot(filtered.reshape(INPUTS * SPEC, FRAME), table, preferred_element_type=jnp.float32)
    chan = chan.astype(jnp.bfloat16).reshape(INPUTS, SPEC, CH).astype(jnp.float32)
    weights = kernel.astype(jnp.bfloat16).astype(jnp.float32)
    half = (KERNEL - 1) // 2
    row_block = min(64, INPUTS)

    def one_block(start):
        rows = lax.dynamic_slice_in_dim(chan, start, row_block, 0)
        vis = jnp.einsum('isc,jsc->cij', rows, chan) * (1.0 / jnp.sqrt(jnp.float32(SPEC)))
        vis = lax.optimization_barrier(vis.astype(jnp.bfloat16)).astype(jnp.float32)
        padded = jnp.pad(vis, ((half, half), (0, 0), (0, 0)))
        total = jnp.zeros_like(vis)
        for step in range(KERNEL):
            total = total + weights[step] * padded[step:step + CH]
        return total.astype(jnp.bfloat16)
    starts = jnp.arange(0, INPUTS, row_block, dtype=jnp.int32)
    result = lax.map(one_block, starts)
    return result.transpose(1, 0, 2, 3).reshape(CH, INPUTS, INPUTS)
```

```python
import functools

import jax
import jax.numpy as jnp
import ml_dtypes
import numpy as np
from jax import lax
from jax.experimental import pallas as pl
from jax.experimental.pallas import tpu as pltpu
from jax.sharding import PartitionSpec as P

NT = (((1,), (1,)), ((), ()))


def make_table(frame, channels, devices):
    order = np.arange(channels).reshape(devices, channels // devices // 2, 2)
    order = order.transpose(2, 0, 1).reshape(-1)
    rows = np.arange(frame)
    phase = (2 * rows[None, :] + 1 + channels) * (2 * order[:, None] + 1) % (8 * channels)
    angle = phase.astype(np.float32) * np.float32(np.pi / (4.0 * channels))
    scale = np.float32(1.0) / np.sqrt(np.float32(channels))
    return (np.cos(angle) * scale).astype(ml_dtypes.bfloat16)


def correlate(
    n, chunks, volts, taps, kernel, table, out,
    frames, framesb, product, chan_f, chan_send, chan_recv, vis_send, vis_recv, rows_f, planes, window,
    send1, recv1, send2, recv2,
):
    groups = lax.axis_index("groups")
    me = lax.axis_index("freq")
    ntaps, frame = taps.shape
    channels = table.shape[0]
    inp, samples = volts.shape
    spectra = samples // frame - ntaps + 1
    pairs = channels // n // 2
    step = pairs // chunks
    inputs = n * inp
    half = channels // 2

    barrier = pltpu.get_barrier_semaphore()

    def greet(p, _):
        pl.semaphore_signal(
            barrier, inc=1, device_id=(groups, lax.rem(me + p, n)),
            device_id_type=pl.DeviceIdType.MESH,
        )
        return 0

    lax.fori_loop(1, n, greet, 0)

    def filter_lanes(mb, _):
        base = pl.multiple_of(mb * 128, 128)
        weights = [jnp.broadcast_to(taps[t : t + 1, pl.ds(base, 128)], (inp, 128)) for t in range(ntaps)]

        def block(s):
            at = pl.multiple_of(s * frame + base, 128)
            return volts[:, pl.ds(at, 128)].astype(jnp.float32)

        held = [block(s) for s in range(ntaps - 1)]
        for s in range(spectra):
            held.append(block(s + ntaps - 1))
            total = weights[0] * held[0]
            for t in range(1, ntaps):
                total = total + weights[t] * held[t]
            frames.at[mb][pl.ds(s, inp, stride=spectra), :] = total
            held = held[1:]
        return 0

    lax.fori_loop(0, frame // 128, filter_lanes, 0)
    for mb in range(frame // 128):
        framesb[:, mb * 128 : (mb + 1) * 128] = frames[mb].astype(jnp.bfloat16)

    product[...] = lax.dot_general(table[...], framesb[...], NT, preferred_element_type=jnp.float32)
    low = lax.broadcasted_iota(jnp.int32, (half, 128), 1) < spectra
    for p in range(inp // 2):
        even = product[:half, 128 * p : 128 * (p + 1)]
        odd = product[half:, 128 * p : 128 * (p + 1)]
        chan_f[pl.ds(2 * p, half, stride=inp), :] = jnp.where(low, even, pltpu.roll(odd, spectra, 1))
        chan_f[pl.ds(2 * p + 1, half, stride=inp), :] = jnp.where(low, pltpu.roll(even, spectra, 1), odd)
    chan_send[...] = chan_f[...].reshape(n, pairs, inp, 128).astype(jnp.bfloat16)

    def copy1(c, peer, source):
        at = pl.ds(c * step, step)
        return pltpu.make_async_remote_copy(
            src_ref=chan_send.at[peer, at], dst_ref=chan_recv.at[source, at],
            send_sem=send1.at[c, peer], recv_sem=recv1.at[c, source],
            device_id=(groups, peer), device_id_type=pl.DeviceIdType.MESH,
        )

    def copy2(c, peer, source):
        at = pl.ds(2 * c * step, 2 * step)
        return pltpu.make_async_remote_copy(
            src_ref=vis_send.at[peer, at], dst_ref=vis_recv.at[source, at],
            send_sem=send2.at[c, peer], recv_sem=recv2.at[c, source],
            device_id=(groups, peer), device_id_type=pl.DeviceIdType.MESH,
        )

    def each_peer(act):
        def body(p, _):
            act(lax.rem(me + p, n))
            return 0

        lax.fori_loop(1, n, body, 0)

    pl.semaphore_wait(barrier, n - 1)
    for c in range(chunks):
        each_peer(lambda peer: copy1(c, peer, me).start())
    chan_recv[me] = chan_send[me]

    count = kernel.shape[1]
    reach = (count - 1) // 2
    window[...] = jnp.zeros_like(window)
    window[0:1, 0:count] = kernel[...].astype(jnp.bfloat16).astype(jnp.float32)
    spread = jnp.broadcast_to(window[0:1, :], (128, 256))
    band = pltpu.roll(spread, 64 - reach, 1, stride=1, stride_axis=0).astype(jnp.bfloat16)

    scale = 1.0 / (spectra**0.5)
    lane = lax.broadcasted_iota(jnp.int32, (inputs, 128), 1)
    for c in range(chunks):
        each_peer(lambda peer: copy1(c, peer, peer).wait_recv())

        def gram(k, _):
            both = chan_recv[:, k].astype(jnp.float32).reshape(inputs, 128)
            right = both.astype(jnp.bfloat16)
            for parity in range(2):
                left = jnp.where((lane < spectra) == (parity == 0), both, 0.0).astype(jnp.bfloat16)
                vis = lax.dot_general(left, right, NT, preferred_element_type=jnp.float32) * scale
                vis_send[:, 2 * k + parity] = vis.reshape(n, inp, inputs).astype(jnp.bfloat16)
            return 0

        lax.fori_loop(c * step, (c + 1) * step, gram, 0)
        each_peer(lambda peer: copy2(c, peer, me).start())
    vis_recv[me] = vis_send[me]
    for c in range(chunks):
        each_peer(lambda peer: copy2(c, peer, peer).wait_recv())

    planes[0:64, :] = jnp.zeros((64, inp * 128), jnp.bfloat16)
    planes[64 + channels :, :] = jnp.zeros((64, inp * 128), jnp.bfloat16)

    def smooth(j, _):
        lanes = pl.ds(pl.multiple_of(j * 128, 128), 128)
        rows_f[...] = vis_recv[:, :, :, lanes].astype(jnp.float32).reshape(channels * inp, 128)
        for i in range(inp):
            planes[64 : 64 + channels, i * 128 : (i + 1) * 128] = (
                rows_f[pl.ds(i, channels, stride=inp), :].astype(jnp.bfloat16)
            )
        for r in range(channels // 128):
            done = jnp.dot(band, planes[r * 128 : r * 128 + 256, :], preferred_element_type=jnp.float32)
            for i in range(inp):
                rows_f[pl.ds(r * 128 * inp + i, 128, stride=inp), :] = done[:, i * 128 : (i + 1) * 128]
        out[:, :, lanes] = rows_f[...].reshape(channels, inp, 128).astype(jnp.bfloat16)
        return 0

    lax.fori_loop(0, inputs // 128, smooth, 0)
    for c in range(chunks):
        each_peer(lambda peer: copy1(c, peer, me).wait_send())
        each_peer(lambda peer: copy2(c, peer, me).wait_send())


def shards(volts, filter_taps, kernel):
    inp, samples = volts.shape
    ntaps, frame = filter_taps.shape
    channels = frame // 2
    spectra = samples // frame - ntaps + 1
    n = lax.axis_size("freq")
    ch_dev = channels // n
    pairs = ch_dev // 2
    inputs = n * inp
    chunks = min(4, pairs)
    table = jnp.asarray(make_table(frame, channels, n))
    vmem = pl.BlockSpec(memory_space=pltpu.VMEM)
    bf16, f32 = jnp.bfloat16, jnp.float32
    return pl.pallas_call(
        functools.partial(correlate, n, chunks),
        out_shape=jax.ShapeDtypeStruct((channels, inp, inputs), bf16),
        in_specs=[vmem] * 4,
        out_specs=vmem,
        scratch_shapes=[
            pltpu.VMEM((frame // 128, inp * spectra, 128), f32),
            pltpu.VMEM((inp * spectra, frame), bf16),
            pltpu.VMEM((channels, inp * spectra), f32),
            pltpu.VMEM((channels // 2 * inp, 128), f32),
            pltpu.VMEM((n, pairs, inp, 128), bf16),
            pltpu.VMEM((n, pairs, inp, 128), bf16),
            pltpu.VMEM((n, ch_dev, inp, inputs), bf16),
            pltpu.VMEM((n, ch_dev, inp, inputs), bf16),
            pltpu.VMEM((channels * inp, 128), f32),
            pltpu.VMEM((channels + 128, inp * 128), bf16),
            pltpu.VMEM((8, 256), f32),
            pltpu.SemaphoreType.DMA((chunks, n)),
            pltpu.SemaphoreType.DMA((chunks, n)),
            pltpu.SemaphoreType.DMA((chunks, n)),
            pltpu.SemaphoreType.DMA((chunks, n)),
        ],
        compiler_params=pltpu.CompilerParams(
            collective_id=0, has_side_effects=True, vmem_limit_bytes=56 << 20
        ),
        name="correlate",
    )(volts, filter_taps, kernel.reshape(1, -1), table)


def solution(mesh):
    return jax.shard_map(
        shards,
        mesh=mesh,
        in_specs=(P(("groups", "freq"), None), P(), P()),
        out_specs=P(None, ("groups", "freq"), None),
        check_vma=False,
    )
```

```python
import functools

import jax
import jax.numpy as jnp
import ml_dtypes
import numpy as np
from jax import lax
from jax.experimental import pallas as pl
from jax.experimental.pallas import tpu as pltpu
from jax.sharding import PartitionSpec as P

NT = (((1,), (1,)), ((), ()))


def make_table(frame, channels, devices):
    order = np.arange(channels).reshape(devices, channels // devices // 2, 2)
    order = order.transpose(2, 0, 1).reshape(-1)
    rows = np.arange(frame)
    phase = (2 * rows[None, :] + 1 + channels) * (2 * order[:, None] + 1) % (8 * channels)
    angle = phase.astype(np.float32) * np.float32(np.pi / (4.0 * channels))
    scale = np.float32(1.0) / np.sqrt(np.float32(channels))
    return (np.cos(angle) * scale).astype(ml_dtypes.bfloat16)


def correlate(
    n, chunks, volts, taps, kernel, table, out,
    frames, framesb, product, chan_f, chan_send, chan_recv, chan_half,
    vis_send, half_send, cross_send, vis, packed, rows_f, planes, window,
    sent, got_chan, got_half, got_vis, got_packed,
):
    groups = lax.axis_index("groups")
    me = lax.axis_index("freq")
    m = n // 2
    side = lax.div(me, m)
    place = lax.rem(me, m)
    ntaps, frame = taps.shape
    channels = table.shape[0]
    inp, samples = volts.shape
    spectra = samples // frame - ntaps + 1
    pairs = channels // n // 2
    step = pairs // chunks
    inputs = n * inp
    half = channels // 2

    barrier = pltpu.get_barrier_semaphore()

    def greet(p, _):
        pl.semaphore_signal(
            barrier, inc=1, device_id=(groups, lax.rem(me + p, n)),
            device_id_type=pl.DeviceIdType.MESH,
        )
        return 0

    lax.fori_loop(1, n, greet, 0)

    def filter_lanes(mb, _):
        base = pl.multiple_of(mb * 128, 128)
        weights = [jnp.broadcast_to(taps[t : t + 1, pl.ds(base, 128)], (inp, 128)) for t in range(ntaps)]

        def block(s):
            at = pl.multiple_of(s * frame + base, 128)
            return volts[:, pl.ds(at, 128)].astype(jnp.float32)

        held = [block(s) for s in range(ntaps - 1)]
        for s in range(spectra):
            held.append(block(s + ntaps - 1))
            total = weights[0] * held[0]
            for t in range(1, ntaps):
                total = total + weights[t] * held[t]
            frames.at[mb][pl.ds(s, inp, stride=spectra), :] = total
            held = held[1:]
        return 0

    lax.fori_loop(0, frame // 128, filter_lanes, 0)
    for mb in range(frame // 128):
        framesb[:, mb * 128 : (mb + 1) * 128] = frames[mb].astype(jnp.bfloat16)

    product[...] = lax.dot_general(table[...], framesb[...], NT, preferred_element_type=jnp.float32)
    low = lax.broadcasted_iota(jnp.int32, (half, 128), 1) < spectra
    for p in range(inp // 2):
        even = product[:half, 128 * p : 128 * (p + 1)]
        odd = product[half:, 128 * p : 128 * (p + 1)]
        chan_f[pl.ds(2 * p, half, stride=inp), :] = jnp.where(low, even, pltpu.roll(odd, spectra, 1))
        chan_f[pl.ds(2 * p + 1, half, stride=inp), :] = jnp.where(low, pltpu.roll(even, spectra, 1), odd)
    chan_send[...] = chan_f[...].reshape(n, pairs, inp, 128).astype(jnp.bfloat16)

    def remote(src, dst, send_sem, recv_sem, peer):
        return pltpu.make_async_remote_copy(
            src_ref=src, dst_ref=dst, send_sem=send_sem, recv_sem=recv_sem,
            device_id=(groups, peer), device_id_type=pl.DeviceIdType.MESH,
        )

    def full_chan(c, peer, source):
        at = pl.ds(c * step, step)
        owner = 2 * lax.rem(peer, m) + lax.div(peer, m)
        return remote(
            chan_send.at[owner, at], chan_recv.at[source, at],
            sent.at[0, c, peer], got_chan.at[c, source], peer,
        )

    def half_chan(c, spot, source):
        at = pl.ds(c * step, step)
        return remote(
            chan_send.at[2 * spot + 1 - side, at], chan_half.at[source, at],
            sent.at[1, c, spot], got_half.at[c, source], side * m + spot,
        )

    def full_vis(c, spot, source):
        at = pl.ds(c * step, step)
        return remote(
            vis_send.at[spot, at], vis.at[source, side, at],
            sent.at[2, c, spot], got_vis.at[c, source], side * m + spot,
        )

    def half_vis(c, spot, source):
        at = pl.ds(c * step, step)
        return remote(
            half_send.at[spot, at], packed.at[side, source, at],
            sent.at[3, c, spot], got_packed.at[0, c, source], side * m + spot,
        )

    def cross_vis(c, spot, source, column_side):
        at = pl.ds(c * step, step)
        return remote(
            cross_send.at[spot, at], packed.at[column_side, source, at],
            sent.at[4, c, spot], got_packed.at[1, c, source], (1 - side) * m + spot,
        )

    def loop(first, act):
        def body(p, _):
            act(lax.rem(place + p, m))
            return 0

        lax.fori_loop(first, m, body, 0)

    pl.semaphore_wait(barrier, n - 1)
    for c in range(chunks):
        loop(0, lambda spot: full_chan(c, (1 - side) * m + spot, me).start())
        loop(1, lambda spot: full_chan(c, side * m + spot, me).start())
        loop(1, lambda spot: half_chan(c, spot, place).start())
    chan_recv[me] = chan_send[2 * place + side]
    chan_half[place] = chan_send[2 * place + 1 - side]

    count = kernel.shape[1]
    reach = (count - 1) // 2
    window[...] = jnp.zeros_like(window)
    window[0:1, 0:count] = kernel[...].astype(jnp.bfloat16).astype(jnp.float32)
    spread = jnp.broadcast_to(window[0:1, :], (128, 256))
    band = pltpu.roll(spread, 64 - reach, 1, stride=1, stride_axis=0).astype(jnp.bfloat16)

    scale = 1.0 / (spectra**0.5)
    ours = inputs // 2
    first = lax.broadcasted_iota(jnp.int32, (ours, 128), 1) < spectra
    lower = lax.broadcasted_iota(jnp.int32, (pairs, inp, inputs), 2) < ours

    def rows_of(value):
        return value.astype(jnp.float32).reshape(-1, 128)

    def product_of(left, right):
        return lax.dot_general(left, right, NT, preferred_element_type=jnp.float32) * scale

    def parities(value):
        return [
            jnp.where(first, value, 0.0).astype(jnp.bfloat16),
            jnp.where(first, 0.0, value).astype(jnp.bfloat16),
        ]

    for c in range(chunks):
        loop(0, lambda spot: full_chan(c, me, (1 - side) * m + spot).wait_recv())
        loop(1, lambda spot: full_chan(c, me, side * m + spot).wait_recv())
        loop(1, lambda spot: half_chan(c, place, spot).wait_recv())

        def gram(k, _):
            every = rows_of(chan_recv[:, k]).astype(jnp.bfloat16)
            own = parities(rows_of(chan_recv[pl.ds(side * m, m), k]))
            other = rows_of(chan_recv[pl.ds((1 - side) * m, m), k]).astype(jnp.bfloat16)
            cross = product_of(other, jnp.concatenate(own, axis=0))
            cross_send[:, k] = cross.reshape(m, inp, inputs).astype(jnp.bfloat16)
            for parity in range(2):
                full = product_of(own[parity], every)
                vis_send[:, k, parity] = full.reshape(m, inp, inputs).astype(jnp.bfloat16)
            mine = rows_of(chan_half[:, k])
            within = product_of(mine.astype(jnp.bfloat16), jnp.concatenate(parities(mine), axis=0))
            half_send[:, k] = within.reshape(m, inp, inputs).astype(jnp.bfloat16)
            return 0

        lax.fori_loop(c * step, (c + 1) * step, gram, 0)
        loop(0, lambda spot: cross_vis(c, spot, place, side).start())
        loop(1, lambda spot: full_vis(c, spot, place).start())
        loop(1, lambda spot: half_vis(c, spot, place).start())
    vis[place, side] = vis_send[place]
    packed[side, place] = half_send[place]
    for c in range(chunks):
        loop(0, lambda spot: cross_vis(c, place, spot, 1 - side).wait_recv())
        loop(1, lambda spot: full_vis(c, place, spot).wait_recv())
        loop(1, lambda spot: half_vis(c, place, spot).wait_recv())

    def unpack(spot, _):
        left = packed[0, spot].astype(jnp.float32)
        right = packed[1, spot].astype(jnp.float32)
        vis[spot, 1 - side, :, 0] = jnp.where(lower, left, pltpu.roll(right, ours, 2)).astype(jnp.bfloat16)
        vis[spot, 1 - side, :, 1] = jnp.where(lower, pltpu.roll(left, ours, 2), right).astype(jnp.bfloat16)
        return 0

    lax.fori_loop(0, m, unpack, 0)

    planes[0:64, :] = jnp.zeros((64, inp * 128), jnp.bfloat16)
    planes[64 + channels :, :] = jnp.zeros((64, inp * 128), jnp.bfloat16)

    def smooth(j, _):
        lanes = pl.ds(pl.multiple_of(j * 128, 128), 128)
        rows_f[...] = vis[:, :, :, :, :, lanes].astype(jnp.float32).reshape(channels * inp, 128)
        for i in range(inp):
            planes[64 : 64 + channels, i * 128 : (i + 1) * 128] = (
                rows_f[pl.ds(i, channels, stride=inp), :].astype(jnp.bfloat16)
            )
        for r in range(channels // 128):
            done = jnp.dot(band, planes[r * 128 : r * 128 + 256, :], preferred_element_type=jnp.float32)
            for i in range(inp):
                rows_f[pl.ds(r * 128 * inp + i, 128, stride=inp), :] = done[:, i * 128 : (i + 1) * 128]
        out[:, :, lanes] = rows_f[...].reshape(channels, inp, 128).astype(jnp.bfloat16)
        return 0

    lax.fori_loop(0, inputs // 128, smooth, 0)
    for c in range(chunks):
        loop(0, lambda spot: full_chan(c, (1 - side) * m + spot, me).wait_send())
        loop(1, lambda spot: full_chan(c, side * m + spot, me).wait_send())
        loop(1, lambda spot: half_chan(c, spot, place).wait_send())
        loop(0, lambda spot: cross_vis(c, spot, place, side).wait_send())
        loop(1, lambda spot: full_vis(c, spot, place).wait_send())
        loop(1, lambda spot: half_vis(c, spot, place).wait_send())


def shards(volts, filter_taps, kernel):
    inp, samples = volts.shape
    ntaps, frame = filter_taps.shape
    channels = frame // 2
    spectra = samples // frame - ntaps + 1
    n = lax.axis_size("freq")
    ch_dev = channels // n
    pairs = ch_dev // 2
    inputs = n * inp
    chunks = min(4, pairs)
    table = jnp.asarray(make_table(frame, channels, n))
    vmem = pl.BlockSpec(memory_space=pltpu.VMEM)
    bf16, f32 = jnp.bfloat16, jnp.float32
    return pl.pallas_call(
        functools.partial(correlate, n, chunks),
        out_shape=jax.ShapeDtypeStruct((channels, inp, inputs), bf16),
        in_specs=[vmem] * 4,
        out_specs=vmem,
        scratch_shapes=[
            pltpu.VMEM((frame // 128, inp * spectra, 128), f32),
            pltpu.VMEM((inp * spectra, frame), bf16),
            pltpu.VMEM((channels, inp * spectra), f32),
            pltpu.VMEM((channels // 2 * inp, 128), f32),
            pltpu.VMEM((n, pairs, inp, 128), bf16),
            pltpu.VMEM((n, pairs, inp, 128), bf16),
            pltpu.VMEM((n // 2, pairs, inp, 128), bf16),
            pltpu.VMEM((n // 2, pairs, 2, inp, inputs), bf16),
            pltpu.VMEM((n // 2, pairs, inp, inputs), bf16),
            pltpu.VMEM((n // 2, pairs, inp, inputs), bf16),
            pltpu.VMEM((n // 2, 2, pairs, 2, inp, inputs), bf16),
            pltpu.VMEM((2, n // 2, pairs, inp, inputs), bf16),
            pltpu.VMEM((channels * inp, 128), f32),
            pltpu.VMEM((channels + 128, inp * 128), bf16),
            pltpu.VMEM((8, 256), f32),
            pltpu.SemaphoreType.DMA((5, chunks, n)),
            pltpu.SemaphoreType.DMA((chunks, n)),
            pltpu.SemaphoreType.DMA((chunks, n // 2)),
            pltpu.SemaphoreType.DMA((chunks, n // 2)),
            pltpu.SemaphoreType.DMA((2, chunks, n // 2)),
        ],
        compiler_params=pltpu.CompilerParams(
            collective_id=0, has_side_effects=True, vmem_limit_bytes=56 << 20
        ),
        name="correlate",
    )(volts, filter_taps, kernel.reshape(1, -1), table)


def solution(mesh):
    return jax.shard_map(
        shards,
        mesh=mesh,
        in_specs=(P(("groups", "freq"), None), P(), P()),
        out_specs=P(None, ("groups", "freq"), None),
        check_vma=False,
    )
```

```python
import functools

import jax
import jax.numpy as jnp
import ml_dtypes
import numpy as np
from jax import lax
from jax.experimental import pallas as pl
from jax.experimental.pallas import tpu as pltpu
from jax.sharding import PartitionSpec as P

NT = (((1,), (1,)), ((), ()))


def make_table(frame, channels, devices):
    order = np.arange(channels).reshape(devices, channels // devices // 2, 2)
    order = order.transpose(2, 0, 1).reshape(-1)
    rows = np.arange(frame)
    phase = (2 * rows[None, :] + 1 + channels) * (2 * order[:, None] + 1) % (8 * channels)
    angle = phase.astype(np.float32) * np.float32(np.pi / (4.0 * channels))
    scale = np.float32(1.0) / np.sqrt(np.float32(channels))
    return (np.cos(angle) * scale).astype(ml_dtypes.bfloat16)


def correlate(
    n, chunks, volts_hbm, taps, kernel, table_hbm, out,
    volts, table,
    frames, framesb, product, chan_f, chan_send, chan_recv, chan_half,
    vis_send, half_send, cross_send, vis, packed, rows_f, planes, window,
    sent, got, fetched,
):
    groups = lax.axis_index("groups")
    me = lax.axis_index("freq")
    m = n // 2
    side = lax.div(me, m)
    place = lax.rem(me, m)
    ntaps, frame = taps.shape
    channels = table.shape[0]
    inp, samples = volts.shape
    spectra = samples // frame - ntaps + 1
    pairs = channels // n // 2
    step = pairs // chunks
    inputs = n * inp
    half = channels // 2

    barrier = pltpu.get_barrier_semaphore()

    def greet(p, _):
        pl.semaphore_signal(
            barrier, inc=1, device_id=(groups, lax.rem(me + p, n)),
            device_id_type=pl.DeviceIdType.MESH,
        )
        return 0

    lax.fori_loop(1, n, greet, 0)

    fetch = [
        pltpu.make_async_copy(volts_hbm, volts, fetched.at[0]),
        pltpu.make_async_copy(table_hbm, table, fetched.at[1]),
    ]
    for copy in fetch:
        copy.start()
    fetch[0].wait()

    def filter_lanes(mb, _):
        base = pl.multiple_of(mb * 128, 128)
        weights = [jnp.broadcast_to(taps[t : t + 1, pl.ds(base, 128)], (inp, 128)) for t in range(ntaps)]

        def block(s):
            at = pl.multiple_of(s * frame + base, 128)
            return volts[:, pl.ds(at, 128)].astype(jnp.float32)

        held = [block(s) for s in range(ntaps - 1)]
        for s in range(spectra):
            held.append(block(s + ntaps - 1))
            total = weights[0] * held[0]
            for t in range(1, ntaps):
                total = total + weights[t] * held[t]
            frames.at[mb][pl.ds(s, inp, stride=spectra), :] = total
            held = held[1:]
        return 0

    lax.fori_loop(0, frame // 128, filter_lanes, 0)
    for mb in range(frame // 128):
        framesb[:, mb * 128 : (mb + 1) * 128] = frames[mb].astype(jnp.bfloat16)

    fetch[1].wait()
    product[...] = lax.dot_general(table[...], framesb[...], NT, preferred_element_type=jnp.float32)
    low = lax.broadcasted_iota(jnp.int32, (half, 128), 1) < spectra
    for p in range(inp // 2):
        even = product[:half, 128 * p : 128 * (p + 1)]
        odd = product[half:, 128 * p : 128 * (p + 1)]
        chan_f[pl.ds(2 * p, half, stride=inp), :] = jnp.where(low, even, pltpu.roll(odd, spectra, 1))
        chan_f[pl.ds(2 * p + 1, half, stride=inp), :] = jnp.where(low, pltpu.roll(even, spectra, 1), odd)
    chan_send[...] = chan_f[...].reshape(n, pairs, inp, 128).astype(jnp.bfloat16)

    def remote(src, dst, send_sem, recv_sem, peer):
        return pltpu.make_async_remote_copy(
            src_ref=src, dst_ref=dst, send_sem=send_sem, recv_sem=recv_sem,
            device_id=(groups, peer), device_id_type=pl.DeviceIdType.MESH,
        )

    def arrived(whole, kind, c):
        remote(whole, whole, sent.at[kind], got.at[kind, c], (1 - side) * m + place).wait_recv()

    def departed(whole, kind):
        remote(whole, whole, sent.at[kind], got.at[kind, 0], (1 - side) * m + place).wait_send()

    def full_chan(c, peer, source):
        at = pl.ds(c * step, step)
        owner = 2 * lax.rem(peer, m) + lax.div(peer, m)
        return remote(
            chan_send.at[owner, at], chan_recv.at[source, at],
            sent.at[0], got.at[0, c], peer,
        )

    def half_chan(c, spot, source):
        at = pl.ds(c * step, step)
        return remote(
            chan_send.at[2 * spot + 1 - side, at], chan_half.at[source, at],
            sent.at[1], got.at[1, c], side * m + spot,
        )

    def full_vis(c, spot, source):
        at = pl.ds(c * step, step)
        return remote(
            vis_send.at[spot, at], vis.at[source, side, at],
            sent.at[2], got.at[2, c], side * m + spot,
        )

    def half_vis(c, spot, source):
        at = pl.ds(c * step, step)
        return remote(
            half_send.at[spot, at], packed.at[side, source, at],
            sent.at[3], got.at[3, c], side * m + spot,
        )

    def cross_vis(c, spot, source, column_side):
        at = pl.ds(c * step, step)
        return remote(
            cross_send.at[spot, at], packed.at[column_side, source, at],
            sent.at[4], got.at[4, c], (1 - side) * m + spot,
        )

    def loop(first, act):
        def body(p, _):
            act(lax.rem(place + p, m))
            return 0

        lax.fori_loop(first, m, body, 0)

    pl.semaphore_wait(barrier, n - 1)
    for c in range(chunks):
        loop(0, lambda spot: full_chan(c, (1 - side) * m + spot, me).start())
        loop(1, lambda spot: full_chan(c, side * m + spot, me).start())
        loop(1, lambda spot: half_chan(c, spot, place).start())
    chan_recv[me] = chan_send[2 * place + side]
    chan_half[place] = chan_send[2 * place + 1 - side]

    count = kernel.shape[1]
    reach = (count - 1) // 2
    window[...] = jnp.zeros_like(window)
    window[0:1, 0:count] = kernel[...].astype(jnp.bfloat16).astype(jnp.float32)
    spread = jnp.broadcast_to(window[0:1, :], (128, 256))
    band = pltpu.roll(spread, 64 - reach, 1, stride=1, stride_axis=0).astype(jnp.bfloat16)

    scale = 1.0 / (spectra**0.5)
    ours = inputs // 2
    first = lax.broadcasted_iota(jnp.int32, (ours, 128), 1) < spectra
    lower = lax.broadcasted_iota(jnp.int32, (pairs, inp, inputs), 2) < ours

    def rows_of(value):
        return value.astype(jnp.float32).reshape(-1, 128)

    def product_of(left, right):
        return lax.dot_general(left, right, NT, preferred_element_type=jnp.float32) * scale

    def parities(value):
        return [
            jnp.where(first, value, 0.0).astype(jnp.bfloat16),
            jnp.where(first, 0.0, value).astype(jnp.bfloat16),
        ]

    for c in range(chunks):
        at = pl.ds(c * step, step)
        arrived(chan_recv.at[pl.ds(0, n - 1), at], 0, c)
        arrived(chan_half.at[pl.ds(0, m - 1), at], 1, c)

        def gram(k, _):
            every = rows_of(chan_recv[:, k]).astype(jnp.bfloat16)
            own = parities(rows_of(chan_recv[pl.ds(side * m, m), k]))
            other = rows_of(chan_recv[pl.ds((1 - side) * m, m), k]).astype(jnp.bfloat16)
            cross = product_of(other, jnp.concatenate(own, axis=0))
            cross_send[:, k] = cross.reshape(m, inp, inputs).astype(jnp.bfloat16)
            for parity in range(2):
                full = product_of(own[parity], every)
                vis_send[:, k, parity] = full.reshape(m, inp, inputs).astype(jnp.bfloat16)
            mine = rows_of(chan_half[:, k])
            within = product_of(mine.astype(jnp.bfloat16), jnp.concatenate(parities(mine), axis=0))
            half_send[:, k] = within.reshape(m, inp, inputs).astype(jnp.bfloat16)
            return 0

        lax.fori_loop(c * step, (c + 1) * step, gram, 0)
        loop(0, lambda spot: cross_vis(c, spot, place, side).start())
        loop(1, lambda spot: full_vis(c, spot, place).start())
        loop(1, lambda spot: half_vis(c, spot, place).start())
    vis[place, side] = vis_send[place]
    packed[side, place] = half_send[place]
    for c in range(chunks):
        at = pl.ds(c * step, step)
        arrived(vis.at[pl.ds(0, m - 1), side, at], 2, c)
        arrived(packed.at[side, pl.ds(0, m - 1), at], 3, c)
        arrived(packed.at[1 - side, pl.ds(0, m), at], 4, c)

    def unpack(spot, _):
        left = packed[0, spot].astype(jnp.float32)
        right = packed[1, spot].astype(jnp.float32)
        vis[spot, 1 - side, :, 0] = jnp.where(lower, left, pltpu.roll(right, ours, 2)).astype(jnp.bfloat16)
        vis[spot, 1 - side, :, 1] = jnp.where(lower, pltpu.roll(left, ours, 2), right).astype(jnp.bfloat16)
        return 0

    lax.fori_loop(0, m, unpack, 0)

    planes[0:64, :] = jnp.zeros((64, inp * 128), jnp.bfloat16)
    planes[64 + channels :, :] = jnp.zeros((64, inp * 128), jnp.bfloat16)

    def smooth(j, _):
        lanes = pl.ds(pl.multiple_of(j * 128, 128), 128)
        rows_f[...] = vis[:, :, :, :, :, lanes].astype(jnp.float32).reshape(channels * inp, 128)
        for i in range(inp):
            planes[64 : 64 + channels, i * 128 : (i + 1) * 128] = (
                rows_f[pl.ds(i, channels, stride=inp), :].astype(jnp.bfloat16)
            )
        for r in range(channels // 128):
            done = jnp.dot(band, planes[r * 128 : r * 128 + 256, :], preferred_element_type=jnp.float32)
            for i in range(inp):
                rows_f[pl.ds(r * 128 * inp + i, 128, stride=inp), :] = done[:, i * 128 : (i + 1) * 128]
        out[:, :, lanes] = rows_f[...].reshape(channels, inp, 128).astype(jnp.bfloat16)
        return 0

    lax.fori_loop(0, inputs // 128, smooth, 0)
    departed(chan_send.at[pl.ds(0, n - 1)], 0)
    departed(chan_send.at[pl.ds(0, m - 1)], 1)
    departed(vis_send.at[pl.ds(0, m - 1)], 2)
    departed(half_send.at[pl.ds(0, m - 1)], 3)
    departed(cross_send.at[pl.ds(0, m)], 4)


def shards(volts, filter_taps, kernel):
    inp, samples = volts.shape
    ntaps, frame = filter_taps.shape
    channels = frame // 2
    spectra = samples // frame - ntaps + 1
    n = lax.axis_size("freq")
    ch_dev = channels // n
    pairs = ch_dev // 2
    inputs = n * inp
    chunks = min(2, pairs)
    table = jnp.asarray(make_table(frame, channels, n))
    vmem = pl.BlockSpec(memory_space=pltpu.VMEM)
    hbm = pl.BlockSpec(memory_space=pl.ANY)
    bf16, f32 = jnp.bfloat16, jnp.float32
    return pl.pallas_call(
        functools.partial(correlate, n, chunks),
        out_shape=jax.ShapeDtypeStruct((channels, inp, inputs), bf16),
        in_specs=[hbm, vmem, vmem, hbm],
        out_specs=vmem,
        scratch_shapes=[
            pltpu.VMEM(volts.shape, bf16),
            pltpu.VMEM(table.shape, bf16),
            pltpu.VMEM((frame // 128, inp * spectra, 128), f32),
            pltpu.VMEM((inp * spectra, frame), bf16),
            pltpu.VMEM((channels, inp * spectra), f32),
            pltpu.VMEM((channels // 2 * inp, 128), f32),
            pltpu.VMEM((n, pairs, inp, 128), bf16),
            pltpu.VMEM((n, pairs, inp, 128), bf16),
            pltpu.VMEM((n // 2, pairs, inp, 128), bf16),
            pltpu.VMEM((n // 2, pairs, 2, inp, inputs), bf16),
            pltpu.VMEM((n // 2, pairs, inp, inputs), bf16),
            pltpu.VMEM((n // 2, pairs, inp, inputs), bf16),
            pltpu.VMEM((n // 2, 2, pairs, 2, inp, inputs), bf16),
            pltpu.VMEM((2, n // 2, pairs, inp, inputs), bf16),
            pltpu.VMEM((channels * inp, 128), f32),
            pltpu.VMEM((channels + 128, inp * 128), bf16),
            pltpu.VMEM((8, 256), f32),
            pltpu.SemaphoreType.DMA((5,)),
            pltpu.SemaphoreType.DMA((5, chunks)),
            pltpu.SemaphoreType.DMA((2,)),
        ],
        compiler_params=pltpu.CompilerParams(
            collective_id=0, has_side_effects=True, vmem_limit_bytes=56 << 20
        ),
        name="correlate",
    )(volts, filter_taps, kernel.reshape(1, -1), table)


def solution(mesh):
    return jax.shard_map(
        shards,
        mesh=mesh,
        in_specs=(P(("groups", "freq"), None), P(), P()),
        out_specs=P(None, ("groups", "freq"), None),
        check_vma=False,
    )
```

```python
import functools

import jax
import jax.numpy as jnp
import ml_dtypes
import numpy as np
from jax import lax
from jax.experimental import pallas as pl
from jax.experimental.pallas import tpu as pltpu
from jax.sharding import PartitionSpec as P

NT = (((1,), (1,)), ((), ()))


def make_table(frame, channels, devices):
    order = np.arange(channels).reshape(devices, channels // devices // 2, 2)
    order = order.transpose(2, 0, 1).reshape(-1)
    rows = np.arange(frame)
    phase = (2 * rows[None, :] + 1 + channels) * (2 * order[:, None] + 1) % (8 * channels)
    angle = phase.astype(np.float32) * np.float32(np.pi / (4.0 * channels))
    scale = np.float32(1.0) / np.sqrt(np.float32(channels))
    return (np.cos(angle) * scale).astype(ml_dtypes.bfloat16)


def correlate(
    n, chunks, volts_hbm, taps, kernel, table_hbm, out_hbm,
    volts, table,
    frames, framesb, product, chan_f, chan_send, chan_recv, chan_half,
    vis_send, half_send, cross_send, vis, packed, rows_f, planes, window, out,
    sent, got, fetched, stored,
):
    groups = lax.axis_index("groups")
    me = lax.axis_index("freq")
    m = n // 2
    side = lax.div(me, m)
    place = lax.rem(me, m)
    ntaps, frame = taps.shape
    channels = table.shape[0]
    inp, samples = volts.shape
    spectra = samples // frame - ntaps + 1
    pairs = channels // n // 2
    step = pairs // chunks
    inputs = n * inp
    half = channels // 2

    barrier = pltpu.get_barrier_semaphore()

    def greet(p, _):
        pl.semaphore_signal(
            barrier, inc=1, device_id=(groups, lax.rem(me + p, n)),
            device_id_type=pl.DeviceIdType.MESH,
        )
        return 0

    lax.fori_loop(1, n, greet, 0)

    fetch = [
        pltpu.make_async_copy(volts_hbm, volts, fetched.at[0]),
        pltpu.make_async_copy(table_hbm, table, fetched.at[1]),
    ]
    for copy in fetch:
        copy.start()
    fetch[0].wait()

    def filter_lanes(mb, _):
        base = pl.multiple_of(mb * 128, 128)
        weights = [jnp.broadcast_to(taps[t : t + 1, pl.ds(base, 128)], (inp, 128)) for t in range(ntaps)]

        def block(s):
            at = pl.multiple_of(s * frame + base, 128)
            return volts[:, pl.ds(at, 128)].astype(jnp.float32)

        held = [block(s) for s in range(ntaps - 1)]
        for s in range(spectra):
            held.append(block(s + ntaps - 1))
            total = weights[0] * held[0]
            for t in range(1, ntaps):
                total = total + weights[t] * held[t]
            frames.at[mb][pl.ds(s, inp, stride=spectra), :] = total
            held = held[1:]
        return 0

    lax.fori_loop(0, frame // 128, filter_lanes, 0)
    for mb in range(frame // 128):
        framesb[:, mb * 128 : (mb + 1) * 128] = frames[mb].astype(jnp.bfloat16)

    fetch[1].wait()
    product[...] = lax.dot_general(table[...], framesb[...], NT, preferred_element_type=jnp.float32)
    low = lax.broadcasted_iota(jnp.int32, (half, 128), 1) < spectra
    for p in range(inp // 2):
        even = product[:half, 128 * p : 128 * (p + 1)]
        odd = product[half:, 128 * p : 128 * (p + 1)]
        chan_f[pl.ds(2 * p, half, stride=inp), :] = jnp.where(low, even, pltpu.roll(odd, spectra, 1))
        chan_f[pl.ds(2 * p + 1, half, stride=inp), :] = jnp.where(low, pltpu.roll(even, spectra, 1), odd)
    chan_send[...] = chan_f[...].reshape(n, pairs, inp, 128).astype(jnp.bfloat16)

    def remote(src, dst, send_sem, recv_sem, peer):
        return pltpu.make_async_remote_copy(
            src_ref=src, dst_ref=dst, send_sem=send_sem, recv_sem=recv_sem,
            device_id=(groups, peer), device_id_type=pl.DeviceIdType.MESH,
        )

    def arrived(whole, kind, c):
        remote(whole, whole, sent.at[kind], got.at[kind, c], (1 - side) * m + place).wait_recv()

    def departed(whole, kind):
        remote(whole, whole, sent.at[kind], got.at[kind, 0], (1 - side) * m + place).wait_send()

    def full_chan(c, peer, source):
        at = pl.ds(c * step, step)
        owner = 2 * lax.rem(peer, m) + lax.div(peer, m)
        return remote(
            chan_send.at[owner, at], chan_recv.at[source, at],
            sent.at[0], got.at[0, c], peer,
        )

    def half_chan(c, spot, source):
        at = pl.ds(c * step, step)
        return remote(
            chan_send.at[2 * spot + 1 - side, at], chan_half.at[source, at],
            sent.at[1], got.at[1, c], side * m + spot,
        )

    def full_vis(c, spot, source):
        at = pl.ds(c * step, step)
        return remote(
            vis_send.at[spot, at], vis.at[source, side, at],
            sent.at[2], got.at[2, c], side * m + spot,
        )

    def half_vis(c, spot, source):
        at = pl.ds(c * step, step)
        return remote(
            half_send.at[spot, at], packed.at[side, source, at],
            sent.at[3], got.at[3, c], side * m + spot,
        )

    def cross_vis(c, spot, source, column_side):
        at = pl.ds(c * step, step)
        return remote(
            cross_send.at[spot, at], packed.at[column_side, source, at],
            sent.at[4], got.at[4, c], (1 - side) * m + spot,
        )

    def loop(first, act):
        def body(p, _):
            act(lax.rem(place + p, m))
            return 0

        lax.fori_loop(first, m, body, 0)

    pl.semaphore_wait(barrier, n - 1)
    for c in range(chunks):
        loop(0, lambda spot: full_chan(c, (1 - side) * m + spot, me).start())
        loop(1, lambda spot: full_chan(c, side * m + spot, me).start())
        loop(1, lambda spot: half_chan(c, spot, place).start())
    chan_recv[me] = chan_send[2 * place + side]
    chan_half[place] = chan_send[2 * place + 1 - side]

    count = kernel.shape[1]
    reach = (count - 1) // 2
    window[...] = jnp.zeros_like(window)
    window[0:1, 0:count] = kernel[...].astype(jnp.bfloat16).astype(jnp.float32)
    spread = jnp.broadcast_to(window[0:1, :], (128, 256))
    band = pltpu.roll(spread, 64 - reach, 1, stride=1, stride_axis=0).astype(jnp.bfloat16)

    scale = 1.0 / (spectra**0.5)
    ours = inputs // 2
    first = lax.broadcasted_iota(jnp.int32, (ours, 128), 1) < spectra
    lower = lax.broadcasted_iota(jnp.int32, (step, inp, inputs), 2) < ours

    def rows_of(value):
        return value.astype(jnp.float32).reshape(-1, 128)

    def product_of(left, right):
        return lax.dot_general(left, right, NT, preferred_element_type=jnp.float32) * scale

    def parities(value):
        return [
            jnp.where(first, value, 0.0).astype(jnp.bfloat16),
            jnp.where(first, 0.0, value).astype(jnp.bfloat16),
        ]

    for c in range(chunks):
        at = pl.ds(c * step, step)
        arrived(chan_recv.at[pl.ds(0, n - 1), at], 0, c)
        arrived(chan_half.at[pl.ds(0, m - 1), at], 1, c)

        def gram(k, _):
            every = rows_of(chan_recv[:, k]).astype(jnp.bfloat16)
            own = parities(rows_of(chan_recv[pl.ds(side * m, m), k]))
            other = rows_of(chan_recv[pl.ds((1 - side) * m, m), k]).astype(jnp.bfloat16)
            cross = product_of(other, jnp.concatenate(own, axis=0))
            cross_send[:, k] = cross.reshape(m, inp, inputs).astype(jnp.bfloat16)
            for parity in range(2):
                full = product_of(own[parity], every)
                vis_send[:, k, parity] = full.reshape(m, inp, inputs).astype(jnp.bfloat16)
            mine = rows_of(chan_half[:, k])
            within = product_of(mine.astype(jnp.bfloat16), jnp.concatenate(parities(mine), axis=0))
            half_send[:, k] = within.reshape(m, inp, inputs).astype(jnp.bfloat16)
            return 0

        lax.fori_loop(c * step, (c + 1) * step, gram, 0)
        loop(0, lambda spot: cross_vis(c, spot, place, side).start())
        loop(1, lambda spot: full_vis(c, spot, place).start())
        loop(1, lambda spot: half_vis(c, spot, place).start())
    vis[place, side] = vis_send[place]
    packed[side, place] = half_send[place]
    for c in range(chunks):
        at = pl.ds(c * step, step)
        arrived(vis.at[pl.ds(0, m - 1), side, at], 2, c)
        arrived(packed.at[side, pl.ds(0, m - 1), at], 3, c)
        arrived(packed.at[1 - side, pl.ds(0, m), at], 4, c)

        def unpack(spot, _):
            left = packed[0, spot, at].astype(jnp.float32)
            right = packed[1, spot, at].astype(jnp.float32)
            even = jnp.where(lower, left, pltpu.roll(right, ours, 2))
            odd = jnp.where(lower, pltpu.roll(left, ours, 2), right)
            vis[spot, 1 - side, at, 0] = even.astype(jnp.bfloat16)
            vis[spot, 1 - side, at, 1] = odd.astype(jnp.bfloat16)
            return 0

        lax.fori_loop(0, m, unpack, 0)

    planes[0:64, :] = jnp.zeros((64, inp * 128), jnp.bfloat16)
    planes[64 + channels :, :] = jnp.zeros((64, inp * 128), jnp.bfloat16)

    def smooth(j, _):
        lanes = pl.ds(pl.multiple_of(j * 128, 128), 128)
        rows_f[...] = vis[:, :, :, :, :, lanes].astype(jnp.float32).reshape(channels * inp, 128)
        for i in range(inp):
            planes[64 : 64 + channels, i * 128 : (i + 1) * 128] = (
                rows_f[pl.ds(i, channels, stride=inp), :].astype(jnp.bfloat16)
            )
        for r in range(channels // 128):
            done = jnp.dot(band, planes[r * 128 : r * 128 + 256, :], preferred_element_type=jnp.float32)
            for i in range(inp):
                rows_f[pl.ds(r * 128 * inp + i, 128, stride=inp), :] = done[:, i * 128 : (i + 1) * 128]
            rows = rows_f[r * 128 * inp : (r + 1) * 128 * inp, :]
            out[r * 128 : (r + 1) * 128, :, lanes] = rows.reshape(128, inp, 128).astype(jnp.bfloat16)
            pltpu.make_async_copy(
                out.at[r * 128 : (r + 1) * 128, :, lanes],
                out_hbm.at[r * 128 : (r + 1) * 128, :, lanes],
                stored.at[0],
            ).start()
        return 0

    lax.fori_loop(0, inputs // 128, smooth, 0)
    departed(chan_send.at[pl.ds(0, n - 1)], 0)
    departed(chan_send.at[pl.ds(0, m - 1)], 1)
    departed(vis_send.at[pl.ds(0, m - 1)], 2)
    departed(half_send.at[pl.ds(0, m - 1)], 3)
    departed(cross_send.at[pl.ds(0, m)], 4)
    pltpu.make_async_copy(out, out_hbm, stored.at[0]).wait()


def shards(volts, filter_taps, kernel):
    inp, samples = volts.shape
    ntaps, frame = filter_taps.shape
    channels = frame // 2
    spectra = samples // frame - ntaps + 1
    n = lax.axis_size("freq")
    ch_dev = channels // n
    pairs = ch_dev // 2
    inputs = n * inp
    chunks = min(2, pairs)
    table = jnp.asarray(make_table(frame, channels, n))
    vmem = pl.BlockSpec(memory_space=pltpu.VMEM)
    hbm = pl.BlockSpec(memory_space=pl.ANY)
    bf16, f32 = jnp.bfloat16, jnp.float32
    return pl.pallas_call(
        functools.partial(correlate, n, chunks),
        out_shape=jax.ShapeDtypeStruct((channels, inp, inputs), bf16),
        in_specs=[hbm, vmem, vmem, hbm],
        out_specs=hbm,
        scratch_shapes=[
            pltpu.VMEM(volts.shape, bf16),
            pltpu.VMEM(table.shape, bf16),
            pltpu.VMEM((frame // 128, inp * spectra, 128), f32),
            pltpu.VMEM((inp * spectra, frame), bf16),
            pltpu.VMEM((channels, inp * spectra), f32),
            pltpu.VMEM((channels // 2 * inp, 128), f32),
            pltpu.VMEM((n, pairs, inp, 128), bf16),
            pltpu.VMEM((n, pairs, inp, 128), bf16),
            pltpu.VMEM((n // 2, pairs, inp, 128), bf16),
            pltpu.VMEM((n // 2, pairs, 2, inp, inputs), bf16),
            pltpu.VMEM((n // 2, pairs, inp, inputs), bf16),
            pltpu.VMEM((n // 2, pairs, inp, inputs), bf16),
            pltpu.VMEM((n // 2, 2, pairs, 2, inp, inputs), bf16),
            pltpu.VMEM((2, n // 2, pairs, inp, inputs), bf16),
            pltpu.VMEM((channels * inp, 128), f32),
            pltpu.VMEM((channels + 128, inp * 128), bf16),
            pltpu.VMEM((8, 256), f32),
            pltpu.VMEM((channels, inp, inputs), bf16),
            pltpu.SemaphoreType.DMA((5,)),
            pltpu.SemaphoreType.DMA((5, chunks)),
            pltpu.SemaphoreType.DMA((2,)),
            pltpu.SemaphoreType.DMA((1,)),
        ],
        compiler_params=pltpu.CompilerParams(
            collective_id=0, has_side_effects=True, vmem_limit_bytes=56 << 20
        ),
        name="correlate",
    )(volts, filter_taps, kernel.reshape(1, -1), table)


def solution(mesh):
    return jax.shard_map(
        shards,
        mesh=mesh,
        in_specs=(P(("groups", "freq"), None), P(), P()),
        out_specs=P(None, ("groups", "freq"), None),
        check_vma=False,
    )
```

```python
import functools

import jax
import jax.numpy as jnp
import ml_dtypes
import numpy as np
from jax import lax
from jax.experimental import pallas as pl
from jax.experimental.pallas import tpu as pltpu
from jax.sharding import PartitionSpec as P

NT = (((1,), (1,)), ((), ()))


def make_table(frame, channels, devices):
    order = np.arange(channels).reshape(devices, channels // devices // 2, 2)
    order = order.transpose(2, 0, 1).reshape(-1)
    rows = np.arange(frame)
    phase = (2 * rows[None, :] + 1 + channels) * (2 * order[:, None] + 1) % (8 * channels)
    angle = phase.astype(np.float32) * np.float32(np.pi / (4.0 * channels))
    scale = np.float32(1.0) / np.sqrt(np.float32(channels))
    return (np.cos(angle) * scale).astype(ml_dtypes.bfloat16)


def correlate(
    n, chunks, volts_hbm, taps, kernel, table_hbm, out_hbm,
    volts, table,
    frames, framesb, product, chan_f, chan_send, chan_recv, chan_half,
    vis_send, half_send, cross_send, vis, packed, rows_f, planes, window, out,
    sent, got, fetched, stored,
):
    groups = lax.axis_index("groups")
    me = lax.axis_index("freq")
    m = n // 2
    side = lax.div(me, m)
    place = lax.rem(me, m)
    ntaps, frame = taps.shape
    channels = table.shape[0]
    inp, samples = volts.shape
    spectra = samples // frame - ntaps + 1
    pairs = channels // n // 2
    step = pairs // chunks
    inputs = n * inp
    half = channels // 2

    barrier = pltpu.get_barrier_semaphore()

    def greet(p, _):
        pl.semaphore_signal(
            barrier, inc=1, device_id=(groups, lax.rem(me + p, n)),
            device_id_type=pl.DeviceIdType.MESH,
        )
        return 0

    lax.fori_loop(1, n, greet, 0)

    fetch = [
        pltpu.make_async_copy(volts_hbm, volts, fetched.at[0]),
        pltpu.make_async_copy(table_hbm, table, fetched.at[1]),
    ]
    for copy in fetch:
        copy.start()
    fetch[0].wait()

    def filter_lanes(mb, _):
        base = pl.multiple_of(mb * 128, 128)
        weights = [jnp.broadcast_to(taps[t : t + 1, pl.ds(base, 128)], (inp, 128)) for t in range(ntaps)]

        def block(s):
            at = pl.multiple_of(s * frame + base, 128)
            return volts[:, pl.ds(at, 128)].astype(jnp.float32)

        held = [block(s) for s in range(ntaps - 1)]
        for s in range(spectra):
            held.append(block(s + ntaps - 1))
            total = weights[0] * held[0]
            for t in range(1, ntaps):
                total = total + weights[t] * held[t]
            frames.at[mb][pl.ds(s, inp, stride=spectra), :] = total
            held = held[1:]
        return 0

    lax.fori_loop(0, frame // 128, filter_lanes, 0)
    for mb in range(frame // 128):
        framesb[:, mb * 128 : (mb + 1) * 128] = frames[mb].astype(jnp.bfloat16)

    fetch[1].wait()
    product[...] = lax.dot_general(table[...], framesb[...], NT, preferred_element_type=jnp.float32)
    low = lax.broadcasted_iota(jnp.int32, (half, 128), 1) < spectra
    for p in range(inp // 2):
        even = product[:half, 128 * p : 128 * (p + 1)]
        odd = product[half:, 128 * p : 128 * (p + 1)]
        chan_f[pl.ds(2 * p, half, stride=inp), :] = jnp.where(low, even, pltpu.roll(odd, spectra, 1))
        chan_f[pl.ds(2 * p + 1, half, stride=inp), :] = jnp.where(low, pltpu.roll(even, spectra, 1), odd)
    chan_send[...] = chan_f[...].reshape(n, pairs, inp, 128).astype(jnp.bfloat16)

    def remote(src, dst, send_sem, recv_sem, peer):
        return pltpu.make_async_remote_copy(
            src_ref=src, dst_ref=dst, send_sem=send_sem, recv_sem=recv_sem,
            device_id=(groups, peer), device_id_type=pl.DeviceIdType.MESH,
        )

    def arrived(whole, kind, c):
        remote(whole, whole, sent.at[kind], got.at[kind, c], (1 - side) * m + place).wait_recv()

    def departed(whole, kind):
        remote(whole, whole, sent.at[kind], got.at[kind, 0], (1 - side) * m + place).wait_send()

    def full_chan(c, peer, source):
        at = pl.ds(c * step, step)
        owner = 2 * lax.rem(peer, m) + lax.div(peer, m)
        return remote(
            chan_send.at[owner, at], chan_recv.at[source, at],
            sent.at[0], got.at[0, c], peer,
        )

    def half_chan(c, spot, source):
        at = pl.ds(c * step, step)
        return remote(
            chan_send.at[2 * spot + 1 - side, at], chan_half.at[source, at],
            sent.at[1], got.at[1, c], side * m + spot,
        )

    def full_vis(c, spot, source):
        at = pl.ds(c * step, step)
        return remote(
            vis_send.at[spot, at], vis.at[source, side, at],
            sent.at[2], got.at[2, c], side * m + spot,
        )

    def half_vis(c, spot, source):
        at = pl.ds(c * step, step)
        return remote(
            half_send.at[spot, at], packed.at[side, source, at],
            sent.at[3], got.at[3, c], side * m + spot,
        )

    def cross_vis(c, spot, source, column_side):
        at = pl.ds(c * step, step)
        return remote(
            cross_send.at[spot, at], packed.at[column_side, source, at],
            sent.at[4], got.at[4, c], (1 - side) * m + spot,
        )

    def loop(first, act):
        def body(p, _):
            act(lax.rem(place + p, m))
            return 0

        lax.fori_loop(first, m, body, 0)

    pl.semaphore_wait(barrier, n - 1)
    for c in range(chunks):
        loop(0, lambda spot: full_chan(c, (1 - side) * m + spot, me).start())
        loop(1, lambda spot: full_chan(c, side * m + spot, me).start())
        loop(1, lambda spot: half_chan(c, spot, place).start())
    chan_recv[me] = chan_send[2 * place + side]
    chan_half[place] = chan_send[2 * place + 1 - side]

    count = kernel.shape[1]
    reach = (count - 1) // 2
    window[...] = jnp.zeros_like(window)
    window[0:1, 0:count] = kernel[...].astype(jnp.bfloat16).astype(jnp.float32)
    spread = jnp.broadcast_to(window[0:1, :], (128, 256))
    band = pltpu.roll(spread, 64 - reach, 1, stride=1, stride_axis=0).astype(jnp.bfloat16)

    planes[0:64, :] = jnp.zeros((64, inp * 128), jnp.bfloat16)
    planes[64 + channels :, :] = jnp.zeros((64, inp * 128), jnp.bfloat16)

    scale = 1.0 / (spectra**0.5)
    ours = inputs // 2
    first = lax.broadcasted_iota(jnp.int32, (ours, 128), 1) < spectra
    lower = lax.broadcasted_iota(jnp.int32, (step, inp, inputs), 2) < ours

    def rows_of(value):
        return value.astype(jnp.float32).reshape(-1, 128)

    def product_of(left, right):
        return lax.dot_general(left, right, NT, preferred_element_type=jnp.float32) * scale

    def parities(value):
        return [
            jnp.where(first, value, 0.0).astype(jnp.bfloat16),
            jnp.where(first, 0.0, value).astype(jnp.bfloat16),
        ]

    for c in range(chunks):
        at = pl.ds(c * step, step)
        arrived(chan_recv.at[pl.ds(0, n - 1), at], 0, c)
        arrived(chan_half.at[pl.ds(0, m - 1), at], 1, c)

        def gram(k, _):
            every = rows_of(chan_recv[:, k]).astype(jnp.bfloat16)
            own = parities(rows_of(chan_recv[pl.ds(side * m, m), k]))
            other = rows_of(chan_recv[pl.ds((1 - side) * m, m), k]).astype(jnp.bfloat16)
            cross = product_of(other, jnp.concatenate(own, axis=0))
            cross_send[:, k] = cross.reshape(m, inp, inputs).astype(jnp.bfloat16)
            for parity in range(2):
                full = product_of(own[parity], every)
                vis_send[:, k, parity] = full.reshape(m, inp, inputs).astype(jnp.bfloat16)
            mine = rows_of(chan_half[:, k])
            within = product_of(mine.astype(jnp.bfloat16), jnp.concatenate(parities(mine), axis=0))
            half_send[:, k] = within.reshape(m, inp, inputs).astype(jnp.bfloat16)
            return 0

        lax.fori_loop(c * step, (c + 1) * step, gram, 0)
        loop(0, lambda spot: cross_vis(c, spot, place, side).start())
        loop(1, lambda spot: full_vis(c, spot, place).start())
        loop(1, lambda spot: half_vis(c, spot, place).start())
    vis[place, side] = vis_send[place]
    packed[side, place] = half_send[place]
    for c in range(chunks):
        at = pl.ds(c * step, step)
        arrived(vis.at[pl.ds(0, m - 1), side, at], 2, c)
        arrived(packed.at[side, pl.ds(0, m - 1), at], 3, c)
        arrived(packed.at[1 - side, pl.ds(0, m), at], 4, c)

        def unpack(spot, _):
            left = packed[0, spot, at].astype(jnp.float32)
            right = packed[1, spot, at].astype(jnp.float32)
            even = jnp.where(lower, left, pltpu.roll(right, ours, 2))
            odd = jnp.where(lower, pltpu.roll(left, ours, 2), right)
            vis[spot, 1 - side, at, 0] = even.astype(jnp.bfloat16)
            vis[spot, 1 - side, at, 1] = odd.astype(jnp.bfloat16)
            return 0

        lax.fori_loop(0, m, unpack, 0)


    def smooth(j, _):
        lanes = pl.ds(pl.multiple_of(j * 128, 128), 128)
        rows_f[...] = vis[:, :, :, :, :, lanes].astype(jnp.float32).reshape(channels * inp, 128)
        for i in range(inp):
            planes[64 : 64 + channels, i * 128 : (i + 1) * 128] = (
                rows_f[pl.ds(i, channels, stride=inp), :].astype(jnp.bfloat16)
            )
        for r in range(channels // 128):
            done = jnp.dot(band, planes[r * 128 : r * 128 + 256, :], preferred_element_type=jnp.float32)
            for i in range(inp):
                rows_f[pl.ds(r * 128 * inp + i, 128, stride=inp), :] = done[:, i * 128 : (i + 1) * 128]
            rows = rows_f[r * 128 * inp : (r + 1) * 128 * inp, :]
            out[r * 128 : (r + 1) * 128, :, lanes] = rows.reshape(128, inp, 128).astype(jnp.bfloat16)
            pltpu.make_async_copy(
                out.at[r * 128 : (r + 1) * 128, :, lanes],
                out_hbm.at[r * 128 : (r + 1) * 128, :, lanes],
                stored.at[0],
            ).start()
        return 0

    lax.fori_loop(0, inputs // 128, smooth, 0)
    departed(chan_send.at[pl.ds(0, n - 1)], 0)
    departed(chan_send.at[pl.ds(0, m - 1)], 1)
    departed(vis_send.at[pl.ds(0, m - 1)], 2)
    departed(half_send.at[pl.ds(0, m - 1)], 3)
    departed(cross_send.at[pl.ds(0, m)], 4)
    pltpu.make_async_copy(out, out_hbm, stored.at[0]).wait()


def shards(volts, filter_taps, kernel):
    inp, samples = volts.shape
    ntaps, frame = filter_taps.shape
    channels = frame // 2
    spectra = samples // frame - ntaps + 1
    n = lax.axis_size("freq")
    ch_dev = channels // n
    pairs = ch_dev // 2
    inputs = n * inp
    chunks = min(2, pairs)
    table = jnp.asarray(make_table(frame, channels, n))
    vmem = pl.BlockSpec(memory_space=pltpu.VMEM)
    hbm = pl.BlockSpec(memory_space=pl.ANY)
    bf16, f32 = jnp.bfloat16, jnp.float32
    return pl.pallas_call(
        functools.partial(correlate, n, chunks),
        out_shape=jax.ShapeDtypeStruct((channels, inp, inputs), bf16),
        in_specs=[hbm, vmem, vmem, hbm],
        out_specs=hbm,
        scratch_shapes=[
            pltpu.VMEM(volts.shape, bf16),
            pltpu.VMEM(table.shape, bf16),
            pltpu.VMEM((frame // 128, inp * spectra, 128), f32),
            pltpu.VMEM((inp * spectra, frame), bf16),
            pltpu.VMEM((channels, inp * spectra), f32),
            pltpu.VMEM((channels // 2 * inp, 128), f32),
            pltpu.VMEM((n, pairs, inp, 128), bf16),
            pltpu.VMEM((n, pairs, inp, 128), bf16),
            pltpu.VMEM((n // 2, pairs, inp, 128), bf16),
            pltpu.VMEM((n // 2, pairs, 2, inp, inputs), bf16),
            pltpu.VMEM((n // 2, pairs, inp, inputs), bf16),
            pltpu.VMEM((n // 2, pairs, inp, inputs), bf16),
            pltpu.VMEM((n // 2, 2, pairs, 2, inp, inputs), bf16),
            pltpu.VMEM((2, n // 2, pairs, inp, inputs), bf16),
            pltpu.VMEM((channels * inp, 128), f32),
            pltpu.VMEM((channels + 128, inp * 128), bf16),
            pltpu.VMEM((8, 256), f32),
            pltpu.VMEM((channels, inp, inputs), bf16),
            pltpu.SemaphoreType.DMA((5,)),
            pltpu.SemaphoreType.DMA((5, chunks)),
            pltpu.SemaphoreType.DMA((2,)),
            pltpu.SemaphoreType.DMA((1,)),
        ],
        compiler_params=pltpu.CompilerParams(
            collective_id=0, has_side_effects=True, vmem_limit_bytes=56 << 20
        ),
        name="correlate",
    )(volts, filter_taps, kernel.reshape(1, -1), table)


def solution(mesh):
    return jax.shard_map(
        shards,
        mesh=mesh,
        in_specs=(P(("groups", "freq"), None), P(), P()),
        out_specs=P(None, ("groups", "freq"), None),
        check_vma=False,
    )
```
